32 devices in a mesh: dp: 4 (over y, x), seq: 4 (over z), mp: 2 (over core).
Axes of the slice: x: 2, y: 2, z: 4, core: 2. Of those that a mesh axis runs over, the one named last changes fastest.
Arguments:
- layer_input: bfloat16 [4, 2048, 1600], P('dp', 'seq'), may hold values from -6 to 6
- doc_pos: int32 [4, 2048], P('dp', 'seq'), may hold values from 0 to 1999, as said below
- ln1_gain: bfloat16 [1600], P(('dp', 'seq')), may hold values from 0.25 to 1.75
- ln1_bias: bfloat16 [1600], P(('dp', 'seq')), may hold values from -3 to 3
- w_qkv: bfloat16 [3, 1600, 1536], P(None, ('dp', 'seq'), 'mp')
- b_qkv: bfloat16 [3, 1536], P(None, 'mp'), may hold values from -3 to 3
- w_out: bfloat16 [1536, 1600], P('mp', ('dp', 'seq')), may hold values from -0.625 to 0.625
- b_out: bfloat16 [1600], P(('dp', 'seq')), may hold values from -3 to 3
- ln2_gain: bfloat16 [1600], P(('dp', 'seq')), may hold values from 0.25 to 1.75
- ln2_bias: bfloat16 [1600], P(('dp', 'seq')), may hold values from -3 to 3
- w_fc: bfloat16 [1600, 6400], P(('dp', 'seq'), 'mp'), may hold values from -0.15625 to 0.15625
- b_fc: bfloat16 [6400], P('mp'), may hold values from -3 to 3
- w_proj: bfloat16 [6400, 1600], P('mp', ('dp', 'seq')), may hold values from -0.078125 to 0.078125
- b_proj: bfloat16 [1600], P(('dp', 'seq')), may hold values from -3 to 3
- cotangent: bfloat16 [4, 2048, 1600], P('dp', 'seq'), may hold values from -6 to 6
Outputs:
- layer_output: float32 [4, 2048, 1600], P('dp', 'seq')
- input_grad: float32 [4, 2048, 1600], P('dp', 'seq')
- ln1_gain_grad: float32 [1600], P(('dp', 'seq'))
- ln1_bias_grad: float32 [1600], P(('dp', 'seq'))
- w_qkv_grad: float32 [3, 1600, 1536], P(None, ('dp', 'seq'), 'mp')
- b_qkv_grad: float32 [3, 1536], P(None, 'mp')
- w_out_grad: float32 [1536, 1600], P('mp', ('dp', 'seq'))
- b_out_grad: float32 [1600], P(('dp', 'seq'))
- ln2_gain_grad: float32 [1600], P(('dp', 'seq'))
- ln2_bias_grad: float32 [1600], P(('dp', 'seq'))
- w_fc_grad: float32 [1600, 6400], P(('dp', 'seq'), 'mp')
- b_fc_grad: float32 [6400], P('mp')
- w_proj_grad: float32 [6400, 1600], P('mp', ('dp', 'seq'))
- b_proj_grad: float32 [1600], P(('dp', 'seq'))
The draws below stay inside these ranges and needn't reach their ends.
Inputs may be any that keep to these rules, and one draw needn't show every extreme that they name: Within a sequence, doc_pos counts up by one from token to token and restarts at 0 where a document starts; every sequence starts a document at its first token; documents hold 200 to 2000 tokens except the last of a sequence, which the sequence's end may cut; some document in every draw holds exactly 2000 tokens.
All inputs are finite; a program needn't handle non-finite values.
Results may differ from the reference program's by a relative error of at most 0.019.
Values may be sent and summed in bfloat16 or wider, within the bound.
No kernel may reach another device: no remote copies, remote signals or barrier semaphores. Data moves between devices by JAX's collectives and lax.ppermute only.
A program may use at most 192 MiB of HBM per device.

```python
import jax
import jax.numpy as jnp
from jax import lax

D = 1600
HEADS = 24
HS = 64
FF = 6400
LEN = 2048
DOC_MIN = 200
DOC_MAX = 2000
NDOC = 11
SEQS = 4
HD = 1536


def draw_w_qkv(key, part):
    split_keys = jax.random.split(jax.random.fold_in(key, 11), 1)
    base = jax.random.normal(split_keys[0], (3, D, HEADS * HS), jnp.float32) * D ** (-0.5)
    return base.astype(jnp.bfloat16)


def draw_doc_pos(key, part):
    doc_lens = jax.random.randint(jax.random.fold_in(key, 23), (SEQS, NDOC), DOC_MIN, DOC_MAX + 1)
    doc_lens = doc_lens.at[0, 0].set(DOC_MAX)
    doc_ends = jnp.cumsum(doc_lens, axis=1)
    doc_starts = doc_ends - doc_lens
    tok_pos = jnp.arange(LEN, dtype=jnp.int32)
    covered = doc_starts[:, :, None] <= tok_pos[None, None, :]
    last_start = jnp.max(jnp.where(covered, doc_starts[:, :, None], 0), axis=1)
    return (tok_pos[None, :] - last_start).astype(jnp.int32)


def block_levels(rng, shape, shards, least, high):
    level = 1.0
    for dim, parts in shards:
        draws = jax.random.uniform(jax.random.fold_in(jax.random.fold_in(rng, 6), dim), (parts,), jnp.float32, least / len(shards), high / len(shards))
        level = level * jnp.repeat(jnp.exp(draws), shape[dim] // parts).reshape((-1,) + (1,) * (len(shape) - 1 - dim))
    return level


def bell_draw(own_key, extent, spread, reach, shards=(), held_as=jnp.bfloat16):
    loudness = block_levels(own_key, extent, shards, -0.22, 0.18) if shards else 1.0
    result = jax.random.normal(own_key, extent, jnp.float32) * spread * loudness
    return jnp.minimum(jnp.maximum(result, -reach), reach).astype(held_as)


def setup_inputs(seed: int = 0) -> dict:
    arg_keys = jax.random.split(jax.random.key(seed), 16)
    return {
        "layer_input": bell_draw(arg_keys[0], (SEQS, LEN, D), 1.0, 6.0, ((0, 4), (1, 4))),
        "doc_pos": draw_doc_pos(jax.random.fold_in(arg_keys[15], 71), 0),
        "ln1_gain": jnp.clip(1.0 + 0.15 * jax.random.normal(arg_keys[2], (D,), jnp.float32), 0.25, 1.75).astype(jnp.bfloat16),
        "ln1_bias": bell_draw(arg_keys[3], (D,), 0.5, 3.0, ((0, 16),)),
        "w_qkv": draw_w_qkv(jax.random.fold_in(arg_keys[15], 71), 0),
        "b_qkv": bell_draw(arg_keys[5], (3, HD), 0.5, 3.0, ((1, 2),)),
        "w_out": bell_draw(arg_keys[6], (HD, D), (HD // 16) ** -0.5, 0.625, ((0, 2), (1, 16))),
        "b_out": bell_draw(arg_keys[7], (D,), 0.5, 3.0, ((0, 16),)),
        "ln2_gain": jnp.clip(1.0 + 0.15 * jax.random.normal(arg_keys[8], (D,), jnp.float32), 0.25, 1.75).astype(jnp.bfloat16),
        "ln2_bias": bell_draw(arg_keys[9], (D,), 0.5, 3.0, ((0, 16),)),
        "w_fc": bell_draw(arg_keys[10], (D, FF), D ** -0.5, 0.15625, ((0, 16), (1, 2))),
        "b_fc": bell_draw(arg_keys[11], (FF,), 0.5, 3.0, ((0, 2),)),
        "w_proj": bell_draw(arg_keys[12], (FF, D), FF ** -0.5, 0.078125, ((0, 2), (1, 16))),
        "b_proj": bell_draw(arg_keys[13], (D,), 0.5, 3.0, ((0, 16),)),
        "cotangent": bell_draw(arg_keys[14], (SEQS, LEN, D), 1.0, 6.0, ((0, 4), (1, 4))),
    }


EPS = 1e-05
GELU_C0 = 0.7978845608028654
GELU_C1 = 0.044715
NEG_BIG = -1e+30

def norm_fwd(values, gain, shift):
    row_mean = lax.optimization_barrier(jnp.mean(values, axis=-1, keepdims=True))
    centred = values - row_mean
    row_var = lax.optimization_barrier(jnp.mean(centred * centred, axis=-1, keepdims=True))
    inv_std = lax.rsqrt(row_var + EPS)
    x_hat = centred * inv_std
    return (x_hat * gain + shift, x_hat, inv_std)

def norm_back(d_out, x_hat, inv_std, gain):
    d_hat = d_out * gain
    return inv_std * (d_hat - lax.optimization_barrier(jnp.mean(d_hat, axis=-1, keepdims=True)) - x_hat * lax.optimization_barrier(jnp.mean(d_hat * x_hat, axis=-1, keepdims=True)))

def gelu_pair(pre):
    inner = GELU_C0 * (pre + GELU_C1 * pre * pre * pre)
    tanh_val = jnp.tanh(inner)
    value = 0.5 * pre * (1.0 + tanh_val)
    slope = 0.5 * (1.0 + tanh_val) + 0.5 * pre * (1.0 - tanh_val * tanh_val) * GELU_C0 * (1.0 + 3.0 * GELU_C1 * pre * pre)
    return (value, slope)

def reference(layer_input, doc_pos, ln1_gain, ln1_bias, w_qkv, b_qkv, w_out, b_out, ln2_gain, ln2_bias, w_fc, b_fc, w_proj, b_proj, cotangent):
    f32 = jnp.float32
    bf16 = jnp.bfloat16
    gain_one = ln1_gain.astype(f32)
    shift_one = ln1_bias.astype(f32)
    gain_two = ln2_gain.astype(f32)
    shift_two = ln2_bias.astype(f32)
    q_scale = HS ** (-0.5)
    tok_pos = jnp.arange(LEN, dtype=jnp.int32)

    def one_sequence(carry, inputs):
        seq_in, seq_pos, seq_cot = inputs
        x_full = seq_in.astype(f32)
        normed_one, hat_one, inv_one = norm_fwd(x_full, gain_one, shift_one)
        normed_one = normed_one.astype(bf16)
        projected = jnp.stack([jnp.dot(normed_one, w_qkv[j], preferred_element_type=f32) for j in range(3)]) + b_qkv.astype(f32)[:, None, :]
        queries = (projected[0] * q_scale).astype(bf16).reshape(LEN, HEADS, HS)
        keys_all = projected[1].astype(bf16).reshape(LEN, HEADS, HS)
        values_all = projected[2].astype(bf16).reshape(LEN, HEADS, HS)
        visible = (tok_pos[None, :] <= tok_pos[:, None]) & (tok_pos[:, None] - tok_pos[None, :] <= seq_pos[:, None])
        visible = visible[None]
        raw = jnp.einsum('qhd,khd->hqk', queries.astype(f32), keys_all.astype(f32))
        masked = jnp.where(visible, raw, NEG_BIG)
        row_max = lax.optimization_barrier(jnp.max(masked, axis=-1))
        log_total = row_max + jnp.log(lax.optimization_barrier(jnp.sum(jnp.where(visible, jnp.exp(masked - row_max[..., None]), 0.0), axis=-1)))
        probs = jnp.where(visible, jnp.exp(raw - log_total[..., None]), 0.0)
        probs_b = probs.astype(bf16)
        attended = jnp.einsum('hqk,khd->qhd', probs_b.astype(f32), values_all.astype(f32)).astype(bf16)
        attended_flat = attended.reshape(LEN, HD)
        resid_one = x_full + jnp.dot(attended_flat, w_out, preferred_element_type=f32) + b_out.astype(f32)
        normed_two, hat_two, inv_two = norm_fwd(resid_one, gain_two, shift_two)
        normed_two = normed_two.astype(bf16)
        pre_act = jnp.dot(normed_two, w_fc, preferred_element_type=f32) + b_fc.astype(f32)
        act_val, act_der = gelu_pair(pre_act)
        act_b = act_val.astype(bf16)
        seq_out = resid_one + jnp.dot(act_b, w_proj, preferred_element_type=f32) + b_proj.astype(f32)
        cot_f = seq_cot.astype(f32)
        g_proj_bias = lax.optimization_barrier(jnp.sum(cot_f, axis=0))
        g_proj = jnp.dot(act_b.T, seq_cot, preferred_element_type=f32)
        d_pre = jnp.dot(seq_cot, w_proj.T, preferred_element_type=f32) * act_der
        g_fc_bias = lax.optimization_barrier(jnp.sum(d_pre, axis=0))
        d_pre_b = d_pre.astype(bf16)
        g_fc = jnp.dot(normed_two.T, d_pre_b, preferred_element_type=f32)
        d_normed_two = jnp.dot(d_pre_b, w_fc.T, preferred_element_type=f32)
        g_gain_two = lax.optimization_barrier(jnp.sum(d_normed_two * hat_two, axis=0))
        g_shift_two = lax.optimization_barrier(jnp.sum(d_normed_two, axis=0))
        d_resid = cot_f + norm_back(d_normed_two, hat_two, inv_two, gain_two)
        g_out_bias = lax.optimization_barrier(jnp.sum(d_resid, axis=0))
        d_resid_b = d_resid.astype(bf16)
        g_out = jnp.dot(attended_flat.T, d_resid_b, preferred_element_type=f32)
        d_attended = jnp.dot(d_resid_b, w_out.T, preferred_element_type=f32).astype(bf16).reshape(LEN, HEADS, HS)
        row_delta = lax.optimization_barrier(jnp.sum(d_attended.astype(f32) * attended.astype(f32), axis=-1)).T
        d_probs = jnp.einsum('qhd,khd->hqk', d_attended.astype(f32), values_all.astype(f32))
        d_raw_b = (probs * (d_probs - row_delta[..., None])).astype(bf16)
        d_query = jnp.einsum('hqk,khd->qhd', d_raw_b.astype(f32), keys_all.astype(f32))
        d_key = jnp.einsum('hqk,qhd->khd', d_raw_b.astype(f32), queries.astype(f32))
        d_value = jnp.einsum('hqk,qhd->khd', probs_b.astype(f32), d_attended.astype(f32))
        d_proj = jnp.stack([d_query.reshape(LEN, HD) * q_scale, d_key.reshape(LEN, HD), d_value.reshape(LEN, HD)])
        g_qkv_bias = lax.optimization_barrier(jnp.sum(d_proj, axis=1))
        d_proj_b = d_proj.astype(bf16)
        g_qkv = jnp.stack([jnp.dot(normed_one.T, d_proj_b[j], preferred_element_type=f32) for j in range(3)])
        d_normed_one = jnp.dot(d_proj_b[0], w_qkv[0].T, preferred_element_type=f32)
        d_normed_one = d_normed_one + jnp.dot(d_proj_b[1], w_qkv[1].T, preferred_element_type=f32)
        d_normed_one = d_normed_one + jnp.dot(d_proj_b[2], w_qkv[2].T, preferred_element_type=f32)
        g_gain_one = lax.optimization_barrier(jnp.sum(d_normed_one * hat_one, axis=0))
        g_shift_one = lax.optimization_barrier(jnp.sum(d_normed_one, axis=0))
        seq_dx = d_resid + norm_back(d_normed_one, hat_one, inv_one, gain_one)
        terms = (g_gain_one, g_shift_one, g_qkv, g_qkv_bias, g_out, g_out_bias, g_gain_two, g_shift_two, g_fc, g_fc_bias, g_proj, g_proj_bias)
        carry = tuple((total + term for total, term in zip(carry, terms)))
        return (carry, (seq_out, seq_dx))
    zeros_init = (jnp.zeros((D,), f32), jnp.zeros((D,), f32), jnp.zeros((3, D, HD), f32), jnp.zeros((3, HD), f32), jnp.zeros((HD, D), f32), jnp.zeros((D,), f32), jnp.zeros((D,), f32), jnp.zeros((D,), f32), jnp.zeros((D, FF), f32), jnp.zeros((FF,), f32), jnp.zeros((FF, D), f32), jnp.zeros((D,), f32))
    totals, stacked = lax.scan(one_sequence, zeros_init, (layer_input, doc_pos, cotangent))
    layer_output, input_grad = stacked
    return (layer_output, input_grad, totals[0], totals[1], totals[2], totals[3], totals[4], totals[5], totals[6], totals[7], totals[8], totals[9], totals[10], totals[11])
```

```python
import functools
import math

import jax
import jax.numpy as jnp
from jax import lax
from jax.experimental import pallas as pl
from jax.experimental.layout import Layout, with_layout_constraint
from jax.experimental.pallas import tpu as pltpu
from jax.sharding import PartitionSpec as P

HS = 64


EPS = 1e-05
GELU_C0 = 0.7978845608028654
GELU_C1 = 0.044715
NEG_BIG = -1e30
KEY_BLOCK = 256


def norm_fwd(values, gain, shift):
    row_mean = jnp.mean(values, axis=-1, keepdims=True)
    centred = values - row_mean
    row_var = jnp.mean(centred * centred, axis=-1, keepdims=True)
    inv_std = lax.rsqrt(row_var + EPS)
    x_hat = centred * inv_std
    return (x_hat * gain + shift, x_hat, inv_std)


def norm_back(d_out, x_hat, inv_std, gain):
    d_hat = d_out * gain
    return inv_std * (
        d_hat
        - jnp.mean(d_hat, axis=-1, keepdims=True)
        - x_hat * jnp.mean(d_hat * x_hat, axis=-1, keepdims=True)
    )


def gelu_pair(pre):
    inner = GELU_C0 * (pre + GELU_C1 * pre * pre * pre)
    tanh_val = jnp.tanh(inner)
    value = 0.5 * pre * (1.0 + tanh_val)
    slope = 0.5 * (1.0 + tanh_val) + 0.5 * pre * (1.0 - tanh_val * tanh_val) * GELU_C0 * (
        1.0 + 3.0 * GELU_C1 * pre * pre
    )
    return (value, slope)


def plain_body(
    layer_input,
    doc_pos,
    ln1_gain,
    ln1_bias,
    w_qkv,
    b_qkv,
    w_out,
    b_out,
    ln2_gain,
    ln2_bias,
    w_fc,
    b_fc,
    w_proj,
    b_proj,
    cotangent,
):
    f32 = jnp.float32
    bf16 = jnp.bfloat16
    seq_count, q_rows, width = layer_input.shape
    heads_here = w_qkv.shape[2] // HS
    tokens_here = seq_count * q_rows
    q_scale = HS ** (-0.5)
    head_shape = (seq_count, q_rows, heads_here, HS)
    gathered = (
        lax.all_gather(w_qkv, ("dp", "seq"), axis=1, tiled=True),
        lax.all_gather(w_out, ("dp", "seq"), axis=1, tiled=True),
        lax.all_gather(w_fc, ("dp", "seq"), axis=0, tiled=True),
        lax.all_gather(w_proj, ("dp", "seq"), axis=1, tiled=True),
        lax.all_gather(ln1_gain, ("dp", "seq"), axis=0, tiled=True),
        lax.all_gather(ln1_bias, ("dp", "seq"), axis=0, tiled=True),
        lax.all_gather(b_out, ("dp", "seq"), axis=0, tiled=True),
        lax.all_gather(ln2_gain, ("dp", "seq"), axis=0, tiled=True),
        lax.all_gather(ln2_bias, ("dp", "seq"), axis=0, tiled=True),
        lax.all_gather(b_proj, ("dp", "seq"), axis=0, tiled=True),
    )
    (
        qkv_full,
        out_full,
        fc_full,
        proj_full,
        gain_one_b,
        shift_one_b,
        out_bias_b,
        gain_two_b,
        shift_two_b,
        proj_bias_b,
    ) = gathered
    gain_one = gain_one_b.astype(f32)
    shift_one = shift_one_b.astype(f32)
    gain_two = gain_two_b.astype(f32)
    shift_two = shift_two_b.astype(f32)
    x_flat = layer_input.reshape(tokens_here, width).astype(f32)
    normed_one, hat_one, inv_one = norm_fwd(x_flat, gain_one, shift_one)
    normed_one = normed_one.astype(bf16)
    projected = (
        jnp.einsum("tc,jcd->jtd", normed_one, qkv_full, preferred_element_type=f32)
        + b_qkv.astype(f32)[:, None, :]
    )
    queries = (projected[0] * q_scale).astype(bf16).reshape(head_shape)
    keys_here = projected[1].astype(bf16).reshape(head_shape)
    values_here = projected[2].astype(bf16).reshape(head_shape)
    key_all, value_all = (
        lax.all_gather(keys_here, "seq", axis=1, tiled=True),
        lax.all_gather(values_here, "seq", axis=1, tiled=True),
    )
    seq_len = key_all.shape[1]
    block_len = math.gcd(seq_len, KEY_BLOCK)
    block_count = seq_len // block_len
    block_ids = jnp.arange(block_count, dtype=jnp.int32)
    query_pos = lax.axis_index("seq") * q_rows + jnp.arange(q_rows, dtype=jnp.int32)
    first_key = query_pos[None, :] - doc_pos

    def scores_at(key_src, first_row, size):
        key_blk = lax.dynamic_slice_in_dim(key_src, first_row, size, 1)
        raw = jnp.einsum("sqhd,skhd->shqk", queries, key_blk, preferred_element_type=f32)
        key_pos = first_row + jnp.arange(size, dtype=jnp.int32)
        visible = (key_pos[None, None, :] <= query_pos[None, :, None]) & (
            key_pos[None, None, :] >= first_key[:, :, None]
        )
        return (raw, visible[:, None, :, :], key_blk)

    def total_step(carry, block_id):
        run_max, run_sum = carry
        raw, visible, key_blk = scores_at(key_all, block_id * block_len, block_len)
        masked = jnp.where(visible, raw, NEG_BIG)
        new_max = jnp.maximum(run_max, jnp.max(masked, axis=-1))
        new_sum = run_sum * jnp.exp(run_max - new_max) + jnp.sum(
            jnp.where(visible, jnp.exp(masked - new_max[..., None]), 0.0), axis=-1
        )
        return ((new_max, new_sum), None)

    stat_shape = (seq_count, heads_here, q_rows)
    (run_max, run_sum), unused = lax.scan(
        total_step, (jnp.full(stat_shape, NEG_BIG, f32), jnp.zeros(stat_shape, f32)), block_ids
    )
    log_total = run_max + jnp.log(run_sum)

    def attend_step(acc, block_id):
        first_row = block_id * block_len
        raw, visible, key_blk = scores_at(key_all, first_row, block_len)
        weights = jnp.where(visible, jnp.exp(raw - log_total[..., None]), 0.0).astype(bf16)
        val_blk = lax.dynamic_slice_in_dim(value_all, first_row, block_len, 1)
        return (
            acc + jnp.einsum("shqk,skhd->sqhd", weights, val_blk, preferred_element_type=f32),
            None,
        )

    attended_acc, unused = lax.scan(attend_step, jnp.zeros(head_shape, f32), block_ids)
    attended = attended_acc.astype(bf16)
    attended_flat = attended.reshape(tokens_here, heads_here * HS)
    attn_part = jnp.dot(attended_flat, out_full, preferred_element_type=f32)
    resid_one = x_flat + lax.psum(attn_part, "mp") + out_bias_b.astype(f32)
    normed_two, hat_two, inv_two = norm_fwd(resid_one, gain_two, shift_two)
    normed_two = normed_two.astype(bf16)
    pre_act = jnp.dot(normed_two, fc_full, preferred_element_type=f32) + b_fc.astype(f32)
    act_val, act_der = gelu_pair(pre_act)
    act_b = act_val.astype(bf16)
    mlp_part = jnp.dot(act_b, proj_full, preferred_element_type=f32)
    layer_output = (
        resid_one
        + lax.psum(mlp_part.astype(jnp.bfloat16), "mp").astype(jnp.float32)
        + proj_bias_b.astype(f32)
    )
    qkv_back, out_back, fc_back, proj_back, gain_one_again, gain_two_again = (
        lax.all_gather(w_qkv, ("dp", "seq"), axis=1, tiled=True),
        lax.all_gather(w_out, ("dp", "seq"), axis=1, tiled=True),
        lax.all_gather(w_fc, ("dp", "seq"), axis=0, tiled=True),
        lax.all_gather(w_proj, ("dp", "seq"), axis=1, tiled=True),
        lax.all_gather(ln1_gain, ("dp", "seq"), axis=0, tiled=True),
        lax.all_gather(ln2_gain, ("dp", "seq"), axis=0, tiled=True),
    )
    gain_one_back = gain_one_again.astype(f32)
    gain_two_back = gain_two_again.astype(f32)
    cot_flat = cotangent.reshape(tokens_here, width)
    cot_f = cot_flat.astype(f32)
    g_proj_bias = jnp.sum(cot_f, axis=0)
    g_proj = jnp.dot(act_b.T, cot_flat, preferred_element_type=f32)
    d_pre = jnp.dot(cot_flat, proj_back.T, preferred_element_type=f32) * act_der
    g_fc_bias_part = jnp.sum(d_pre, axis=0)
    d_pre_b = d_pre.astype(bf16)
    g_fc = jnp.dot(normed_two.T, d_pre_b, preferred_element_type=f32)
    d_normed_two = lax.psum(jnp.dot(d_pre_b, fc_back.T, preferred_element_type=f32), "mp")
    g_gain_two = jnp.sum(d_normed_two * hat_two, axis=0)
    g_shift_two = jnp.sum(d_normed_two, axis=0)
    d_resid = cot_f + norm_back(d_normed_two, hat_two, inv_two, gain_two_back)
    g_out_bias = jnp.sum(d_resid, axis=0)
    d_resid_b = d_resid.astype(bf16)
    g_out = jnp.dot(attended_flat.T, d_resid_b, preferred_element_type=f32)
    d_attended = (
        jnp.dot(d_resid_b, out_back.T, preferred_element_type=f32).astype(bf16).reshape(head_shape)
    )
    row_delta = jnp.transpose(
        jnp.sum(d_attended.astype(f32) * attended.astype(f32), axis=-1), (0, 2, 1)
    )
    key_back, value_back = (
        lax.all_gather(keys_here, "seq", axis=1, tiled=True),
        lax.all_gather(values_here, "seq", axis=1, tiled=True),
    )

    def probs_at(first_row, size):
        raw, visible, key_blk = scores_at(key_back, first_row, size)
        probs = jnp.where(visible, jnp.exp(raw - log_total[..., None]), 0.0)
        val_blk = lax.dynamic_slice_in_dim(value_back, first_row, size, 1)
        d_probs = jnp.einsum("sqhd,skhd->shqk", d_attended, val_blk, preferred_element_type=f32)
        d_raw_b = (probs * (d_probs - row_delta[..., None])).astype(bf16)
        return (probs, d_raw_b, key_blk)

    def query_step(acc, block_id):
        probs, d_raw_b, key_blk = probs_at(block_id * block_len, block_len)
        return (
            acc + jnp.einsum("shqk,skhd->sqhd", d_raw_b, key_blk, preferred_element_type=f32),
            None,
        )

    d_query, unused = lax.scan(query_step, jnp.zeros(head_shape, f32), block_ids)
    row_count = lax.axis_size("seq") * q_rows
    sub_len = math.gcd(row_count, KEY_BLOCK)
    sub_count = row_count // sub_len

    def one_sub(sub_id):
        probs, d_raw_b, key_blk = probs_at(sub_id * sub_len, sub_len)
        d_key_blk = jnp.einsum("shqk,sqhd->kshd", d_raw_b, queries, preferred_element_type=f32)
        d_value_blk = jnp.einsum(
            "shqk,sqhd->kshd", probs.astype(bf16), d_attended, preferred_element_type=f32
        )
        return jnp.stack([d_key_blk, d_value_blk], axis=2)

    pieces = lax.map(one_sub, jnp.arange(sub_count, dtype=jnp.int32))
    summed = lax.psum_scatter(
        pieces.reshape(row_count, seq_count, 2, heads_here, HS).astype(jnp.bfloat16),
        "seq",
        scatter_dimension=0,
        tiled=True,
    ).astype(jnp.float32)
    d_key = jnp.transpose(summed[:, :, 0], (1, 0, 2, 3)).reshape(tokens_here, heads_here * HS)
    d_value = jnp.transpose(summed[:, :, 1], (1, 0, 2, 3)).reshape(tokens_here, heads_here * HS)
    d_proj = jnp.stack([d_query.reshape(tokens_here, heads_here * HS) * q_scale, d_key, d_value])
    g_qkv_bias_part = jnp.sum(d_proj, axis=1)
    d_proj_b = d_proj.astype(bf16)
    g_qkv = jnp.einsum("tc,jtd->jcd", normed_one, d_proj_b, preferred_element_type=f32)
    d_normed_one = lax.psum(
        jnp.einsum("jtd,jcd->tc", d_proj_b, qkv_back, preferred_element_type=f32).astype(
            jnp.bfloat16
        ),
        "mp",
    ).astype(jnp.float32)
    g_gain_one = jnp.sum(d_normed_one * hat_one, axis=0)
    g_shift_one = jnp.sum(d_normed_one, axis=0)
    input_grad = d_resid + norm_back(d_normed_one, hat_one, inv_one, gain_one_back)
    g_qkv_bias, g_fc_bias = lax.psum((g_qkv_bias_part, g_fc_bias_part), ("dp", "seq"))
    owned = (
        lax.psum_scatter(g_qkv, ("dp", "seq"), scatter_dimension=1, tiled=True),
        lax.psum_scatter(g_out, ("dp", "seq"), scatter_dimension=1, tiled=True),
        lax.psum_scatter(g_fc, ("dp", "seq"), scatter_dimension=0, tiled=True),
        lax.psum_scatter(g_proj, ("dp", "seq"), scatter_dimension=1, tiled=True),
        lax.psum_scatter(g_gain_one, ("dp", "seq"), scatter_dimension=0, tiled=True),
        lax.psum_scatter(g_shift_one, ("dp", "seq"), scatter_dimension=0, tiled=True),
        lax.psum_scatter(g_out_bias, ("dp", "seq"), scatter_dimension=0, tiled=True),
        lax.psum_scatter(g_gain_two, ("dp", "seq"), scatter_dimension=0, tiled=True),
        lax.psum_scatter(g_shift_two, ("dp", "seq"), scatter_dimension=0, tiled=True),
        lax.psum_scatter(g_proj_bias, ("dp", "seq"), scatter_dimension=0, tiled=True),
    )
    (
        own_qkv,
        own_out,
        own_fc,
        own_proj,
        own_gain_one,
        own_shift_one,
        own_out_bias,
        own_gain_two,
        own_shift_two,
        own_proj_bias,
    ) = owned
    return (
        layer_output.reshape(layer_input.shape),
        input_grad.reshape(layer_input.shape),
        own_gain_one,
        own_shift_one,
        own_qkv,
        g_qkv_bias,
        own_out,
        own_out_bias,
        own_gain_two,
        own_shift_two,
        own_fc,
        g_fc_bias,
        own_proj,
        own_proj_bias,
    )


BLK = 256


def pick(pair, c, cc, q, zz):
    return jnp.where(c == cc, pair[0][q, zz], pair[1][q, zz])


def put(pair, c, cc, q, zz, cols, value):
    @pl.when(c == cc)
    def _():
        pair[0][q, zz, :, cols] = value

    @pl.when(c != cc)
    def _():
        pair[1][q, zz, :, cols] = value


def piece_of(ref, c, i, p):
    cols = ref.shape[0]
    zz = i // (2 * cols)
    return (i // cols) % 2, (i % cols) ^ p, zz


def attend_fwd_kernel(
    n_heads, pos_ref, lo_ref, own_ref, other_ref, fk_ref, out_ref, out2_ref, lse_ref, qk_s, vt_s
):
    f32 = jnp.float32
    cols, blocks, piece, _ = own_ref.shape
    width = n_heads * HS
    p, c = pos_ref[0], pos_ref[1]
    per = BLK // piece
    n_blk = 2 * cols * blocks // per
    pair = (own_ref, other_ref)

    def fill(b, carry):
        at = pl.multiple_of(b * BLK, BLK)
        src = jnp.concatenate(
            [pick(pair, c, *piece_of(own_ref, c, b * per + i, p)) for i in range(per)], axis=0
        )
        for h in range(2 * n_heads):
            qk_s[h, pl.ds(at, BLK), :] = src[:, h * HS : (h + 1) * HS]
        vt = src[:, 2 * width :].T
        for h in range(n_heads):
            vt_s[h, :, pl.ds(at, BLK)] = vt[h * HS : (h + 1) * HS]
        return carry

    lax.fori_loop(0, n_blk, fill, 0)
    iota_q = lax.broadcasted_iota(jnp.int32, (BLK, BLK), 1)
    iota_k = lax.broadcasted_iota(jnp.int32, (BLK, BLK), 0)

    def rows(qi, carry0):
        q0 = pl.multiple_of(qi * BLK, BLK)
        fk = fk_ref[0:1, pl.ds(q0, BLK)]

        def step(kb, carry):
            k0 = pl.multiple_of(kb * BLK, BLK)
            kpos = iota_k + k0
            visible = (kpos >= fk) & (kpos <= iota_q + q0)
            new = []
            scores = [
                lax.dot_general(
                    qk_s[n_heads + h, pl.ds(k0, BLK), :],
                    qk_s[h, pl.ds(q0, BLK), :],
                    (((1,), (1,)), ((), ())),
                    preferred_element_type=f32,
                )
                for h in range(n_heads)
            ]
            for h in range(n_heads):
                m, l, acc = carry[h]
                st = jnp.where(visible, scores[h], NEG_BIG)
                m2 = jnp.maximum(m, jnp.max(st, axis=0, keepdims=True))
                scale = jnp.exp(m - m2)
                pt = jnp.where(visible, jnp.exp(st - m2), 0.0)
                l2 = l * scale + jnp.sum(pt, axis=0, keepdims=True)
                acc2 = acc * scale + jnp.dot(
                    vt_s[h, :, pl.ds(k0, BLK)],
                    pt.astype(jnp.bfloat16),
                    preferred_element_type=f32,
                )
                new.append((m2, l2, acc2))
            return tuple(new)

        init = tuple(
            (
                jnp.full((1, BLK), NEG_BIG, f32),
                jnp.zeros((1, BLK), f32),
                jnp.zeros((HS, BLK), f32),
            )
            for _ in range(n_heads)
        )
        res = lax.fori_loop(lo_ref[qi], qi + 1, step, init)
        for h in range(n_heads):
            m, l, acc = res[h]
            lse_ref[h : h + 1, pl.ds(q0, BLK)] = m + jnp.log(l)
        at = jnp.concatenate([res[h][2] / res[h][1] for h in range(n_heads)], axis=0)
        at = at.T.astype(jnp.bfloat16)
        for i in range(per):
            where = piece_of(own_ref, c, qi * per + i, p)
            put((out_ref, out2_ref), c, *where, slice(None), at[i * piece : (i + 1) * piece])
        return carry0

    lax.fori_loop(0, n_blk, rows, 0)


def attend_bwd_kernel(
    n_heads,
    q_scale,
    pos_ref,
    hi_ref,
    own_ref,
    other_ref,
    fk_ref,
    lse_ref,
    o_ref,
    o2_ref,
    do_ref,
    do2_ref,
    out_ref,
    out2_ref,
    op_s,
    kt_s,
    dlt_s,
    dqt_s,
):
    f32 = jnp.float32
    bf16 = jnp.bfloat16
    cols, blocks, piece, _ = own_ref.shape
    width = n_heads * HS
    p, c = pos_ref[0], pos_ref[1]
    per = BLK // piece
    n_blk = 2 * cols * blocks // per
    outs = (out_ref, out2_ref)

    def fill(b, carry):
        at = pl.multiple_of(b * BLK, BLK)
        places = [piece_of(own_ref, c, b * per + i, p) for i in range(per)]

        def load(pair):
            return jnp.concatenate([pick(pair, c, *w) for w in places], axis=0)

        src = load((own_ref, other_ref))
        dsrc = load((do_ref, do2_ref))
        osrc = load((o_ref, o2_ref))
        for h in range(3 * n_heads):
            op_s[h, pl.ds(at, BLK), :] = src[:, h * HS : (h + 1) * HS]
        for h in range(n_heads):
            op_s[3 * n_heads + h, pl.ds(at, BLK), :] = dsrc[:, h * HS : (h + 1) * HS]
        kt = src[:, width : 2 * width].T
        pt = (dsrc.astype(f32) * osrc.astype(f32)).T
        for h in range(n_heads):
            kt_s[h, :, pl.ds(at, BLK)] = kt[h * HS : (h + 1) * HS]
            dlt_s[h : h + 1, pl.ds(at, BLK)] = jnp.sum(
                pt[h * HS : (h + 1) * HS], axis=0, keepdims=True
            )
        return carry

    lax.fori_loop(0, n_blk, fill, 0)
    dqt_s[...] = jnp.zeros_like(dqt_s)
    iota_q = lax.broadcasted_iota(jnp.int32, (BLK, BLK), 1)
    iota_k = lax.broadcasted_iota(jnp.int32, (BLK, BLK), 0)

    def keys(kb, carry0):
        k0 = pl.multiple_of(kb * BLK, BLK)
        kpos = k0 + iota_k

        def step(qi, carry):
            q0 = pl.multiple_of(qi * BLK, BLK)
            visible = (kpos >= fk_ref[0:1, pl.ds(q0, BLK)]) & (kpos <= iota_q + q0)
            new = []
            for h in range(n_heads):
                dk, dv = carry[h]
                qb = op_s[h, pl.ds(q0, BLK), :]
                dob = op_s[3 * n_heads + h, pl.ds(q0, BLK), :]
                st = lax.dot_general(
                    op_s[n_heads + h, pl.ds(k0, BLK), :],
                    qb,
                    (((1,), (1,)), ((), ())),
                    preferred_element_type=f32,
                )
                pt = jnp.where(visible, jnp.exp(st - lse_ref[h : h + 1, pl.ds(q0, BLK)]), 0.0)
                dpt = lax.dot_general(
                    op_s[2 * n_heads + h, pl.ds(k0, BLK), :],
                    dob,
                    (((1,), (1,)), ((), ())),
                    preferred_element_type=f32,
                )
                dst = (pt * (dpt - dlt_s[h : h + 1, pl.ds(q0, BLK)])).astype(bf16)
                dv = dv + jnp.dot(pt.astype(bf16), dob, preferred_element_type=f32)
                dk = dk + jnp.dot(dst, qb, preferred_element_type=f32)
                dqt_s[h, :, pl.ds(q0, BLK)] += jnp.dot(
                    kt_s[h, :, pl.ds(k0, BLK)], dst, preferred_element_type=f32
                )
                new.append((dk, dv))
            return tuple(new)

        zero = jnp.zeros((BLK, HS), f32)
        res = lax.fori_loop(kb, hi_ref[kb], step, tuple((zero, zero) for _ in range(n_heads)))
        both = jnp.concatenate(
            [res[h][0] for h in range(n_heads)] + [res[h][1] for h in range(n_heads)], axis=1
        ).astype(bf16)
        for i in range(per):
            where = piece_of(own_ref, c, kb * per + i, p)
            value = both[i * piece : (i + 1) * piece]
            put(outs, c, *where, slice(width, 3 * width), value)
        return carry0

    lax.fori_loop(0, n_blk, keys, 0)

    def queries(b, carry0):
        at = pl.multiple_of(b * BLK, BLK)
        dq = jnp.concatenate([dqt_s[h, :, pl.ds(at, BLK)] for h in range(n_heads)], axis=0)
        dq = (dq.T * q_scale).astype(bf16)
        for i in range(per):
            where = piece_of(own_ref, c, b * per + i, p)
            put(outs, c, *where, slice(0, width), dq[i * piece : (i + 1) * piece])
        return carry0

    lax.fori_loop(0, n_blk, queries, 0)


def vmem():
    return pl.BlockSpec(memory_space=pltpu.VMEM)


def smem():
    return pl.BlockSpec(memory_space=pltpu.SMEM)


def attend_forward(n_heads, place, lo, qkv, first_key):
    cols, blocks, piece, _ = qkv[0].shape
    total = 2 * cols * blocks * piece
    out = jax.ShapeDtypeStruct((cols, blocks, piece, n_heads * HS), jnp.bfloat16)
    return pl.pallas_call(
        functools.partial(attend_fwd_kernel, n_heads),
        out_shape=(out, out, jax.ShapeDtypeStruct((8, total), jnp.float32)),
        in_specs=[smem(), smem(), vmem(), vmem(), vmem()],
        out_specs=(vmem(), vmem(), vmem()),
        scratch_shapes=[
            pltpu.VMEM((2 * n_heads, total, HS), jnp.bfloat16),
            pltpu.VMEM((n_heads, HS, total), jnp.bfloat16),
        ],
        compiler_params=pltpu.CompilerParams(vmem_limit_bytes=48 << 20),
        cost_estimate=pl.CostEstimate(
            flops=8 * total * total * n_heads * HS,
            bytes_accessed=4 << 20,
            transcendentals=n_heads * total * total,
        ),
        name="attend_fwd",
    )(place, lo, *qkv, first_key)


def attend_backward(n_heads, q_scale, place, hi, qkv, first_key, lse, attended, d_attended):
    cols, blocks, piece, _ = qkv[0].shape
    total = 2 * cols * blocks * piece
    out = jax.ShapeDtypeStruct(qkv[0].shape, jnp.bfloat16)
    return pl.pallas_call(
        functools.partial(attend_bwd_kernel, n_heads, q_scale),
        out_shape=(out, out),
        in_specs=[smem(), smem()] + [vmem()] * 8,
        out_specs=(vmem(), vmem()),
        scratch_shapes=[
            pltpu.VMEM((4 * n_heads, total, HS), jnp.bfloat16),
            pltpu.VMEM((n_heads, HS, total), jnp.bfloat16),
            pltpu.VMEM((8, total), jnp.float32),
            pltpu.VMEM((n_heads, HS, total), jnp.float32),
        ],
        compiler_params=pltpu.CompilerParams(vmem_limit_bytes=56 << 20),
        cost_estimate=pl.CostEstimate(
            flops=16 * total * total * n_heads * HS,
            bytes_accessed=8 << 20,
            transcendentals=n_heads * total * total,
        ),
        name="attend_bwd",
    )(place, hi, *qkv, first_key, lse, *attended, *d_attended)


def rows_major(value):
    return with_layout_constraint(value, Layout(major_to_minor=tuple(range(value.ndim))))


def flip(value, axis, bits):
    pairs = [(i, i ^ bits) for i in range(lax.axis_size(axis))]
    return rows_major(lax.ppermute(rows_major(value), axis, pairs))


def swap(value, axis):
    return rows_major(lax.all_to_all(rows_major(value), axis, 0, 0, tiled=True))


CHUNK = 32


def row_call(kernel, outs, *ins, name):
    return pl.pallas_call(
        kernel,
        out_shape=tuple(jax.ShapeDtypeStruct(shape, dtype) for shape, dtype in outs),
        in_specs=[vmem()] * len(ins),
        out_specs=tuple(vmem() for _ in outs),
        compiler_params=pltpu.CompilerParams(vmem_limit_bytes=56 << 20),
        cost_estimate=pl.CostEstimate(
            flops=0,
            transcendentals=0,
            bytes_accessed=sum(math.prod(v.shape) * v.dtype.itemsize for v in ins)
            + sum(math.prod(shape) * jnp.dtype(dtype).itemsize for shape, dtype in outs),
        ),
        name=name,
    )(*ins)


def row_loop(rows, step, init=0):
    return lax.fori_loop(
        0, rows // CHUNK, lambda i, carry: step(pl.multiple_of(i * CHUNK, CHUNK), carry), init
    )


def halves_of(ref, start):
    per = ref.shape[1] // CHUNK
    i = start // CHUNK
    return ref[i // per, pl.ds(pl.multiple_of(lax.rem(i, per) * CHUNK, CHUNK), CHUNK), :]


def put_rows(ref, rows, value):
    used = value.shape[1]
    ref[rows, :used] = value
    if ref.shape[1] > used:
        ref[rows, used:] = jnp.zeros((value.shape[0], ref.shape[1] - used), ref.dtype)


def norm_kernel(d, x_ref, vec_ref, u_ref):
    def step(s, carry):
        x = x_ref[pl.ds(s, CHUNK), :d].astype(jnp.float32)
        y, _, _ = norm_fwd(x, vec_ref[0:1, :d], vec_ref[1:2, :d])
        put_rows(u_ref, pl.ds(s, CHUNK), y.astype(jnp.bfloat16))
        return carry

    row_loop(x_ref.shape[0], step)


def join_kernel(*refs):
    out_ref = refs[-1]
    at = 0
    for ref in refs[:-1]:

        def step(s, carry, ref=ref, at=at):
            out_ref[pl.ds(at + s, CHUNK), :] = ref[pl.ds(s, CHUNK), :]
            return carry

        row_loop(ref.shape[0], step)
        at += ref.shape[0]


def first_sum_kernel(part_ref, got_ref, sa_ref, sb_ref, k_ref):
    half = sa_ref.shape[1]
    for k in range(4):
        for side in range(2):

            def step(s, carry, k=k, side=side):
                rows = pl.ds(k * 2 * half + side * half + s, CHUNK)
                v = part_ref[rows, :].astype(jnp.float32) + got_ref[rows, :].astype(jnp.float32)
                here = pl.ds(s, CHUNK)
                if side == 0:
                    if k < 2:
                        k_ref[k, here, :] = v
                    else:
                        sa_ref[k - 2, here, :] = v.astype(jnp.bfloat16)
                elif k % 2 == 0:
                    k_ref[2 + k // 2, here, :] = v
                else:
                    sb_ref[k // 2, here, :] = v.astype(jnp.bfloat16)
                return carry

            row_loop(half, step)


def second_sum_kernel(k_ref, ga_ref, gb_ref, sa_ref, sb_ref, out_ref):
    def step(s, carry):
        here = pl.ds(s, CHUNK)
        f32 = jnp.float32
        out_ref[0, here, :] = k_ref[0, here, :] + ga_ref[0, here, :].astype(f32)
        sa_ref[here, :] = (k_ref[1, here, :] + ga_ref[1, here, :].astype(f32)).astype(jnp.bfloat16)
        out_ref[1, here, :] = k_ref[2, here, :] + gb_ref[0, here, :].astype(f32)
        sb_ref[here, :] = (k_ref[3, here, :] + gb_ref[1, here, :].astype(f32)).astype(jnp.bfloat16)
        return carry

    row_loop(sa_ref.shape[0], step)


def last_sum(d, k_ref, ga_ref, gb_ref, side, here):
    got = ga_ref if side == 0 else gb_ref
    return k_ref[side, here, :d] + got[here, :d].astype(jnp.float32)


def each_half(half, body):
    for side in range(2):

        def step(s, carry, side=side):
            body(side, pl.ds(s, CHUNK), pl.ds(side * half + s, CHUNK))
            return carry

        row_loop(half, step)


def resid_kernel(d, k_ref, ga_ref, gb_ref, x_ref, vec_ref, resid_ref, u_ref):
    def body(side, here, rows):
        v = x_ref[rows, :d].astype(jnp.float32) + last_sum(d, k_ref, ga_ref, gb_ref, side, here)
        v = v + vec_ref[2:3, :d]
        put_rows(resid_ref, rows, v)
        y, _, _ = norm_fwd(v, vec_ref[3:4, :d], vec_ref[4:5, :d])
        put_rows(u_ref, rows, y.astype(jnp.bfloat16))

    each_half(ga_ref.shape[0], body)


def result_kernel(d, k_ref, ga_ref, gb_ref, resid_ref, vec_ref, out_ref):
    def body(side, here, rows):
        v = resid_ref[rows, :d] + last_sum(d, k_ref, ga_ref, gb_ref, side, here)
        put_rows(out_ref, rows, (v + vec_ref[5:6, :d]).astype(jnp.bfloat16))

    each_half(ga_ref.shape[0], body)


def fold(v):
    return jnp.sum(v.reshape(CHUNK // 8, 8, v.shape[-1]), axis=0)


def d_resid_kernel(d, k_ref, ga_ref, gb_ref, resid_ref, cot_ref, vec_ref, d_ref, u_ref, sum_ref):
    f32 = jnp.float32
    sum_ref[...] = jnp.zeros_like(sum_ref)

    def body(side, here, rows):
        dn = last_sum(d, k_ref, ga_ref, gb_ref, side, here)
        _, hat, inv = norm_fwd(resid_ref[rows, :d], vec_ref[3:4, :d], vec_ref[4:5, :d])
        v = cot_ref[rows, :d].astype(f32) + norm_back(dn, hat, inv, vec_ref[3:4, :d])
        put_rows(d_ref, rows, v)
        put_rows(u_ref, rows, v.astype(jnp.bfloat16))
        sum_ref[0] += fold(v)
        sum_ref[1] += fold(dn * hat)
        sum_ref[2] += fold(dn)

    each_half(ga_ref.shape[0], body)


def d_input_kernel(d, k_ref, ga_ref, gb_ref, x_ref, d_ref, vec_ref, out_ref, sum_ref):
    sum_ref[...] = jnp.zeros_like(sum_ref)

    def body(side, here, rows):
        dn = last_sum(d, k_ref, ga_ref, gb_ref, side, here)
        x = x_ref[rows, :d].astype(jnp.float32)
        _, hat, inv = norm_fwd(x, vec_ref[0:1, :d], vec_ref[1:2, :d])
        v = d_ref[rows, :d] + norm_back(dn, hat, inv, vec_ref[0:1, :d])
        put_rows(out_ref, rows, v.astype(jnp.bfloat16))
        sum_ref[0] += fold(dn * hat)
        sum_ref[1] += fold(dn)

    each_half(ga_ref.shape[0], body)


def split_weights_kernel(in_ref, one_ref, two_ref):
    outer, inner, r, _ = in_ref.shape
    w, w2 = one_ref.shape[1], two_ref.shape[1]
    used = outer * inner * r
    for zz in range(outer):
        for pp in range(inner):
            at = (pp * outer + zz) * r
            v = in_ref[zz, pp]
            one_ref[at : at + r, :] = v[:, :w]
            two_ref[at : at + r, :] = v[:, w : w + w2]
    for ref in (one_ref, two_ref):
        if ref.shape[0] > used:
            ref[used:, :] = jnp.zeros((ref.shape[0] - used, ref.shape[1]), ref.dtype)


def join_grads_kernel(r, one_ref, two_ref, vec_ref, out_ref):
    outer, inner, _, _ = out_ref.shape
    w, w2 = one_ref.shape[1], two_ref.shape[1]
    for zz in range(outer):
        for pp in range(inner):
            at = (pp * outer + zz) * r
            out_ref[zz, pp, :r, :w] = one_ref[at : at + r, :]
            out_ref[zz, pp, :r, w : w + w2] = two_ref[at : at + r, :]
            out_ref[zz, pp, r:, :] = vec_ref[zz, pp]
            if out_ref.shape[3] > w + w2:
                tail = (r, out_ref.shape[3] - w - w2)
                out_ref[zz, pp, :r, w + w2 :] = jnp.zeros(tail, out_ref.dtype)


def lanes(width):
    return -(-width // 128) * 128


def dp_rows(own, after=()):
    half = own.shape[0] // 2
    u1, u2 = flip(own, "dp", 1), flip(own, "dp", 2)
    u1, u2, after = lax.optimization_barrier((u1, u2, after))
    a3, b3 = flip(u1[:half], "dp", 2), flip(u2[half:], "dp", 1)
    return (own, u1, u2, a3, b3), after


def both_rows(mine):
    rows = sum(v.shape[0] for v in mine)
    out = [((rows, mine[0].shape[1]), mine[0].dtype)]
    other = tuple(flip(v, "mp", 1) for v in mine)
    return [row_call(join_kernel, out, *v, name="join")[0] for v in (mine, other)]


def gather_rows(own):
    return both_rows(dp_rows(own)[0])


def scatter_rows(parts, finish):
    f32, bf16 = jnp.float32, jnp.bfloat16
    part_own, part_other = parts
    rows, width = part_own.shape
    half = rows // 8
    got = flip(part_other, "mp", 1)
    two, four = ((2, half, width), bf16), ((4, half, width), f32)
    sa, sb, kept = row_call(first_sum_kernel, [two, two, four], part_own, got, name="sum_a")
    ga, gb = flip(sa, "dp", 2), flip(sb, "dp", 1)
    one = ((half, width), bf16)
    sa, sb, kept = row_call(
        second_sum_kernel, [one, one, ((2, half, width), f32)], kept, ga, gb, name="sum_b"
    )
    return finish(kept, flip(sa, "dp", 1), flip(sb, "dp", 2))


def turn_out(rows_in):
    rows, width = rows_in.shape
    v = swap(rows_in.reshape(4, rows // 4, width), "seq")
    return swap(v, "dp").reshape(rows, width)


def both_halves(half_rows):
    other = flip(half_rows, "mp", 1)
    first = lax.axis_index("mp") == 0
    return jnp.concatenate(
        [jnp.where(first, half_rows, other), jnp.where(first, other, half_rows)]
    )


def as_lines(vec):
    return jnp.pad(vec, (0, -vec.shape[0] % 1024)).reshape(-1, 128)


def stack_flips(value, axis):
    me = lax.axis_index(axis)
    out = jnp.zeros((4,) + value.shape, value.dtype)
    for k in range(4):
        part = value if k == 0 else flip(value, axis, k)
        out = lax.dynamic_update_slice_in_dim(out, part[None], me ^ k, 0)
    return out


def send_grads(r, one, two, shared, vectors):
    bf16 = jnp.bfloat16
    wide = lanes(one.shape[1] + two.shape[1])
    extra = -r % 8 or 8
    lines = jnp.broadcast_to(jnp.pad(shared, (0, wide - shared.shape[0])), (4, 4, 1, wide))
    slices = jnp.transpose(vectors.reshape(-1, 4, 4, r), (2, 1, 0, 3)).reshape(4, 4, 1, -1)
    slices = jnp.pad(slices, ((0, 0), (0, 0), (0, extra - 2), (0, wide - slices.shape[3])))
    lines = jnp.concatenate([lines, slices], axis=2).astype(bf16)
    grad = row_call(
        functools.partial(join_grads_kernel, r),
        [((4, 4, r + extra, wide), bf16)],
        one,
        two,
        lines,
        name="join_grads",
    )[0]
    return swap(grad, "seq")


def take_grads(r, got, shared, vectors):
    total = jnp.sum(got.astype(jnp.float32), axis=0).astype(jnp.bfloat16)
    got = swap(total, "dp").astype(jnp.float32)
    heads = jnp.sum(got[:, r + 1, : vectors * r], axis=0).reshape(-1, r)
    return got[:, :r], got[:, r, :shared], heads + flip(heads, "mp", 1)


def sum_lines(vectors, own_rows):
    p, z = lax.axis_index("dp"), lax.axis_index("seq")
    lines = as_lines(vectors.reshape(-1))
    for axis, bits in (("mp", 1), ("dp", 1), ("dp", 2), ("seq", 1), ("seq", 2)):
        lines = lines + flip(lines, axis, bits)
    heads = lines.reshape(-1)[: vectors.size].reshape(vectors.shape[0], 16, own_rows)
    return lax.dynamic_index_in_dim(heads, p * 4 + z, 1, keepdims=False)


def fast_body(
    layer_input,
    doc_pos,
    ln1_gain,
    ln1_bias,
    w_qkv,
    b_qkv,
    w_out,
    b_out,
    ln2_gain,
    ln2_bias,
    w_fc,
    b_fc,
    w_proj,
    b_proj,
    cotangent,
):
    f32 = jnp.float32
    bf16 = jnp.bfloat16
    p, z, c = lax.axis_index("dp"), lax.axis_index("seq"), lax.axis_index("mp")
    n = 4
    _, q_rows, width = layer_input.shape
    half = q_rows // 2
    piece = half // n
    own_rows = w_qkv.shape[1]
    head_w = w_qkv.shape[2] // n
    n_heads = head_w // HS
    hid_w = w_fc.shape[1] // n
    q_scale = HS ** (-0.5)
    tokens = n * q_rows
    nt = (((1,), (1,)), ((), ()))
    tn = (((0,), (0,)), ((), ()))

    wide = lanes(width)

    def half_in(rows):
        v = lax.dynamic_slice_in_dim(rows[0], c * half, half, 0)
        return jnp.pad(v, ((0, 0), (0, wide - width))).reshape(n, piece, wide)

    def calls(kernel):
        return functools.partial(kernel, width)

    small = jnp.concatenate(
        [v.astype(f32) for v in (ln1_gain, ln1_bias, b_out, ln2_gain, ln2_bias, b_proj)]
        + [doc_pos.reshape(-1).astype(f32)]
    )
    used = small.shape[0]
    small = stack_flips(as_lines(small), "seq")
    x_dp = swap(half_in(layer_input), "dp")
    small, x_dp = lax.optimization_barrier((small, x_dp))
    small = stack_flips(small, "dp").reshape(16, -1)
    x_t = swap(x_dp, "seq").reshape(half, wide)

    wq = jnp.transpose(w_qkv.reshape(3, own_rows, n, head_w), (2, 1, 0, 3)).reshape(
        n, own_rows, 3 * head_w
    )
    wo = jnp.transpose(w_out.reshape(n, head_w, own_rows), (0, 2, 1))
    wf = jnp.transpose(w_fc.reshape(own_rows, n, hid_w), (1, 0, 2))
    wp = jnp.transpose(w_proj.reshape(n, hid_w, own_rows), (0, 2, 1))

    def bundle_of(one, two):
        both = jnp.concatenate([one, two], axis=2)
        return jnp.pad(both, ((0, 0), (0, 0), (0, lanes(both.shape[2]) - both.shape[2])))

    def split_up(full, one, two):
        outs = [((wide, v.shape[2]), bf16) for v in (one, two)]
        return row_call(split_weights_kernel, outs, full, name="split_weights")

    bundle, small, x_dp = lax.optimization_barrier((bundle_of(wq, wo), small, x_dp))
    bundle = swap(bundle, "dp")
    bundle, x_t = lax.optimization_barrier((bundle, x_t))
    full = jnp.broadcast_to(bundle[None], (n,) + bundle.shape).reshape(-1, *bundle.shape[1:])
    full = swap(full, "seq").reshape(n, *bundle.shape)

    vecs = jnp.stack(
        [small[:, i * own_rows : (i + 1) * own_rows].reshape(width) for i in range(6)]
        + [jnp.zeros((width,), f32)] * 2
    )
    docs = small[:, 6 * own_rows : used].reshape(4, tokens)
    docs = lax.dynamic_index_in_dim(docs, z, 0, keepdims=False).astype(jnp.int32)
    first_key = jnp.arange(tokens, dtype=jnp.int32) - docs
    n_blk = tokens // BLK
    first_of_blk = first_key.reshape(n_blk, BLK)[:, 0]
    low_blk = first_of_blk // BLK
    high_blk = jnp.sum(
        (low_blk[None, :] <= jnp.arange(n_blk, dtype=jnp.int32)[:, None]).astype(jnp.int32), axis=1
    )
    first_key = jnp.broadcast_to(first_key[None], (8, tokens))
    place = jnp.stack([p, c]).astype(jnp.int32)

    (u_one,) = row_call(calls(norm_kernel), [((half, wide), bf16)], x_t, vecs, name="norm_one")
    mine_one, later = dp_rows(u_one, (half_in(cotangent), bundle_of(wf, wp)))
    cot_dp, bundle_b = swap(later[0], "dp"), swap(later[1], "dp")
    all_one = both_rows(mine_one)
    all_one[0], all_one[1], full, cot_dp = lax.optimization_barrier(
        (all_one[0], all_one[1], full, cot_dp)
    )
    cot_t = swap(cot_dp, "seq").reshape(half, wide)
    qkv_w, out_w = split_up(full, wq, wo)
    qkv_bias = lax.dynamic_slice_in_dim(b_qkv.astype(f32), p * head_w, head_w, 1)
    scales = jnp.repeat(jnp.array([q_scale, 1.0, 1.0], f32), head_w)
    qkv = [
        rows_major(
            (
                (jnp.dot(v, qkv_w, preferred_element_type=f32) + qkv_bias.reshape(-1)) * scales
            ).astype(bf16)
        ).reshape(4, 4, piece, 3 * head_w)
        for v in all_one
    ]
    qkv[0], qkv[1], cot_t, bundle_b = lax.optimization_barrier((qkv[0], qkv[1], cot_t, bundle_b))
    full_b = lax.all_gather(bundle_b, "seq", axis=0)
    att_own, att_other, lse = attend_forward(n_heads, place, low_blk, qkv, first_key)
    mine_cot = (cot_t,) + tuple(flip(cot_t, "dp", k) for k in (1, 2, 3))
    att_own, att_other, mine_cot = lax.optimization_barrier((att_own, att_other, mine_cot))
    attended = [v.reshape(tokens // 2, head_w) for v in (att_own, att_other)]

    def times_t(pair, weight):
        other = lax.dot_general(pair[1], weight, nt, preferred_element_type=f32).astype(bf16)
        own = lax.dot_general(pair[0], weight, nt, preferred_element_type=f32).astype(bf16)
        return rows_major(own), rows_major(other)

    def weight_grad(left, right):
        return rows_major(
            (
                lax.dot_general(left[0], right[0], tn, preferred_element_type=f32)
                + lax.dot_general(left[1], right[1], tn, preferred_element_type=f32)
            ).astype(bf16)
        )

    row_f, row_b = ((half, wide), f32), ((half, wide), bf16)
    resid_one, u_two = scatter_rows(
        times_t(attended, out_w),
        lambda *k: row_call(calls(resid_kernel), [row_f, row_b], *k, x_t, vecs, name="resid"),
    )
    all_two = gather_rows(u_two)
    all_cot = both_rows(mine_cot)
    fc_w, proj_w = split_up(full_b, wf, wp)
    fc_bias = lax.dynamic_slice_in_dim(b_fc.astype(f32), p * hid_w, hid_w, 0)
    act_b, d_pre_b, g_fc_bias = [], [], 0.0
    for i in range(2):
        pre = jnp.dot(all_two[i], fc_w, preferred_element_type=f32) + fc_bias
        act_val, act_der = gelu_pair(pre)
        act_b.append(act_val.astype(bf16))
        d_pre = jnp.dot(all_cot[i], proj_w, preferred_element_type=f32) * act_der
        g_fc_bias = g_fc_bias + jnp.sum(d_pre, axis=0)
        d_pre_b.append(d_pre.astype(bf16))

    two_parts = times_t(d_pre_b, fc_w)
    two_parts, d_pre_b, act_b = lax.optimization_barrier((two_parts, d_pre_b, act_b))
    d_resid, u_res, early_sums = scatter_rows(
        two_parts,
        lambda *k: row_call(
            calls(d_resid_kernel),
            [row_f, row_b, ((3, 8, width), f32)],
            *k,
            resid_one,
            cot_t,
            vecs,
            name="d_resid",
        ),
    )
    cot_sum = jnp.sum(cot_t[:, :width].astype(f32), axis=0)[None]
    got_b = send_grads(
        own_rows, weight_grad(all_two, d_pre_b), weight_grad(all_cot, act_b), g_fc_bias, cot_sum
    )
    mlp_parts = times_t(act_b, proj_w)
    mine_res, mlp_parts = dp_rows(u_res, mlp_parts)
    all_res = both_rows(mine_res)
    (out_t,) = scatter_rows(
        mlp_parts,
        lambda *k: row_call(calls(result_kernel), [row_b], *k, resid_one, vecs, name="result"),
    )

    d_att = [
        rows_major(jnp.dot(v, out_w, preferred_element_type=f32).astype(bf16)).reshape(
            4, 4, piece, head_w
        )
        for v in all_res
    ]
    d_qkv = attend_backward(
        n_heads, q_scale, place, high_blk, qkv, first_key, lse, (att_own, att_other), d_att
    )
    d_qkv, out_t = lax.optimization_barrier((d_qkv, out_t))
    d_qkv = [v.reshape(tokens // 2, 3 * head_w) for v in d_qkv]
    one_parts = times_t(d_qkv, qkv_w)
    one_parts, d_qkv, got_b = lax.optimization_barrier((one_parts, d_qkv, got_b))
    in_t, late_sums = scatter_rows(
        one_parts,
        lambda *k: row_call(
            calls(d_input_kernel), [row_b, ((2, 8, width), f32)], *k, x_t, d_resid, vecs, name="d_input"
        ),
    )
    layer_output = turn_out(out_t)
    own_b, fc_parts, cot_vec = take_grads(own_rows, got_b, hid_w, 1)
    own_fc = jnp.transpose(own_b[:, :, :hid_w], (1, 0, 2)).reshape(own_rows, n * hid_w)
    own_proj = jnp.transpose(own_b[:, :, hid_w : 2 * hid_w], (0, 2, 1)).reshape(
        n * hid_w, own_rows
    )
    qkv_sum = jnp.sum(d_qkv[0].astype(f32), axis=0) + jnp.sum(d_qkv[1].astype(f32), axis=0)
    got_a = send_grads(
        own_rows,
        weight_grad(all_one, d_qkv),
        weight_grad(all_res, attended),
        qkv_sum,
        jnp.sum(early_sums, axis=1),
    )
    got_a, in_t, late_sums = lax.optimization_barrier((got_a, in_t, late_sums))
    input_grad = turn_out(in_t)
    own_a, qkv_parts, early_vecs = take_grads(own_rows, got_a, 3 * head_w, 3)
    own_qkv = jnp.transpose(
        own_a[:, :, : 3 * head_w].reshape(n, own_rows, 3, head_w), (2, 1, 0, 3)
    ).reshape(3, own_rows, n * head_w)
    own_out = jnp.transpose(own_a[:, :, 3 * head_w :], (0, 2, 1)).reshape(n * head_w, own_rows)
    late_vecs = sum_lines(jnp.sum(late_sums, axis=1), own_rows)
    g_qkv_bias = jnp.transpose(qkv_parts.reshape(n, 3, head_w), (1, 0, 2)).reshape(3, n * head_w)
    layer_output = both_halves(layer_output)[:, :width].astype(f32)
    input_grad = both_halves(input_grad)[:, :width].astype(f32)
    return (
        layer_output.reshape(layer_input.shape),
        input_grad.reshape(layer_input.shape),
        late_vecs[0],
        late_vecs[1],
        own_qkv,
        g_qkv_bias,
        own_out,
        early_vecs[0],
        early_vecs[1],
        early_vecs[2],
        own_fc,
        fc_parts.reshape(-1),
        own_proj,
        cot_vec[0],
    )


def fits(layer_input, w_qkv, w_fc):
    n, depth, pair = lax.axis_size("dp"), lax.axis_size("seq"), lax.axis_size("mp")
    seqs, rows, _ = layer_input.shape
    return (
        n == 4
        and depth == n
        and pair == 2
        and seqs == 1
        and rows % (2 * n * 16) == 0
        and BLK % (rows // (2 * n)) == 0
        and (n * rows) % BLK == 0
        and w_qkv.shape[2] % (n * HS) == 0
        and w_fc.shape[1] % n == 0
    )


def body(*args):
    if fits(args[0], args[4], args[10]):
        return fast_body(*args)
    return plain_body(*args)


def solution(mesh):
    return jax.shard_map(
        body,
        mesh=mesh,
        in_specs=(
            P("dp", "seq", None),
            P("dp", "seq"),
            P(("dp", "seq")),
            P(("dp", "seq")),
            P(None, ("dp", "seq"), "mp"),
            P(None, "mp"),
            P("mp", ("dp", "seq")),
            P(("dp", "seq")),
            P(("dp", "seq")),
            P(("dp", "seq")),
            P(("dp", "seq"), "mp"),
            P("mp"),
            P("mp", ("dp", "seq")),
            P(("dp", "seq")),
            P("dp", "seq", None),
        ),
        out_specs=(
            P("dp", "seq", None),
            P("dp", "seq", None),
            P(("dp", "seq")),
            P(("dp", "seq")),
            P(None, ("dp", "seq"), "mp"),
            P(None, "mp"),
            P("mp", ("dp", "seq")),
            P(("dp", "seq")),
            P(("dp", "seq")),
            P(("dp", "seq")),
            P(("dp", "seq"), "mp"),
            P("mp"),
            P("mp", ("dp", "seq")),
            P(("dp", "seq")),
        ),
        check_vma=False,
    )
```
